256 devices in a mesh: tile: 32 (over z, y_hi, core), cam: 8 (over y_lo, x).
Axes of the slice: x: 4, y: 4 (y_hi: 2, y_lo: 2; y = y_hi * 2 + y_lo), z: 8, core: 2. Of those that a mesh axis runs over, the one named last changes fastest.
Arguments:
- features: bfloat16 [6144, 256], P(('tile', 'cam')), may hold values from -6 to 6
- value_weight: bfloat16 [256, 256], replicated, may hold values from -0.375 to 0.375
- output_weight: bfloat16 [256, 256], replicated, may hold values from -0.375 to 0.375
- hit_list: int32 [32, 2], P('tile'), may hold values from 0 to 5, as said below
- sample_index: int32 [16384, 2, 64], P('tile'), may hold values from 0 to 1023, as said below
- attention: bfloat16 [16384, 64], P('tile'), may hold values from 0.0099487305 to 1
- validity: int32 [16384, 2], P('tile'), may hold values from 0 to 1, as said below
Outputs:
- projected: bfloat16 [16384, 256], P(('tile', 'cam'))
The draws below stay inside these ranges and needn't reach their ends.
Inputs may be any that keep to these rules, and one draw needn't show every extreme that they name: `hit_list`: camera numbers 0 to 5; where a tile sees one camera its two entries are equal. `validity`: where a tile's two hit_list entries are equal, the second column is 0 for every query of that tile. `sample_index`: for one query, slot and head, the 8 entries h * 8 to h * 8 + 7 all differ.
All inputs are finite; a program needn't handle non-finite values.
Results may differ from the reference program's by a relative error of at most 0.0058.
Values may be sent and summed in bfloat16 or wider, within the bound.
No kernel may reach another device: no remote copies, remote signals or barrier semaphores. Data moves between devices by JAX's collectives and lax.ppermute only.
A program may use at most 64 MiB of HBM per device.

```python
import math
import jax
import jax.numpy as jnp
from jax import lax

D = 256
H = 8
K = 8
HITS = 2
CAMS = 6
CAM_ROWS = 1024
Q_TILE = 512
TILES = 32
QUERIES = 16384
FEATURE_ROWS = 6144


def camera_pairs(key):
    base_key = jax.random.fold_in(key, 7)
    lead_key, stride_key, lone_key = jax.random.split(base_key, 3)
    leading = jax.random.randint(lead_key, (TILES,), 0, CAMS)
    stride = jax.random.randint(stride_key, (TILES,), 1, CAMS)
    lonely = jax.random.randint(lone_key, (TILES,), 0, 3) == 0
    partner = jnp.where(lonely, leading, (leading + stride) % CAMS)
    return jnp.stack([leading, partner], axis=1).astype(jnp.int32)


def draw_hit_list(key, part):
    return camera_pairs(key)


def draw_validity(key, part):
    pairs = camera_pairs(key)
    query_cams = jnp.repeat(pairs, Q_TILE, axis=0)
    first_key, second_key = jax.random.split(jax.random.fold_in(key, 19))
    leading_live = jax.random.randint(first_key, (QUERIES,), 0, 5) != 0
    second_live = jax.random.randint(second_key, (QUERIES,), 0, 5) < 3
    second_live = second_live & (query_cams[:, 1] != query_cams[:, 0])
    return jnp.stack([leading_live, second_live], axis=1).astype(jnp.int32)


def draw_sample_index(key, part):
    center_key, jitter_key = jax.random.split(jax.random.fold_in(key, 31))
    spacing = CAM_ROWS // K
    center = jax.random.randint(center_key, (QUERIES, HITS, H, 1), 0, CAM_ROWS)
    jitter = jax.random.randint(jitter_key, (QUERIES, HITS, H, K), 0, spacing)
    strides = jnp.arange(K).reshape(1, 1, 1, K) * spacing
    return ((center + strides + jitter) % CAM_ROWS).reshape(QUERIES, HITS, H * K).astype(jnp.int32)


def shard_levels(key, extent, pieces, smallest, high):
    loudness = 1.0
    for dim, blocks in pieces:
        steps = jax.random.uniform(jax.random.fold_in(jax.random.fold_in(key, 6), dim), (blocks,), jnp.float32, smallest / len(pieces), high / len(pieces))
        loudness = loudness * jnp.repeat(jnp.exp(steps), extent[dim] // blocks).reshape((-1,) + (1,) * (len(extent) - 1 - dim))
    return loudness


def normal_values(rng, extent, width, limit, shards=(), kind=jnp.bfloat16):
    entries = width * jax.random.normal(rng, extent, jnp.float32)
    if shards:
        entries = entries * shard_levels(rng, extent, shards, -0.22, 0.18)
    return jnp.clip(entries, -limit, limit).astype(kind)


def setup_inputs(seed: int = 0) -> dict:
    arg_keys = jax.random.split(jax.random.key(seed), 8)
    return {
        "features": normal_values(arg_keys[0], (FEATURE_ROWS, D), 1.0, 6.0, ((0, 256),)),
        "value_weight": normal_values(arg_keys[1], (D, D), D ** -0.5, 0.375),
        "output_weight": normal_values(arg_keys[2], (D, D), D ** -0.5, 0.375),
        "hit_list": draw_hit_list(jax.random.fold_in(arg_keys[7], 71), 0),
        "sample_index": draw_sample_index(jax.random.fold_in(arg_keys[7], 71), 0),
        "attention": jnp.clip(jnp.exp(math.log(1.0) - 4.61031033 * jax.random.uniform(arg_keys[5], (QUERIES, H * K), jnp.float32) ** shard_levels(arg_keys[5], (QUERIES, H * K), ((0, 32),), -0.2, 0.2)), 0.0099487305, 1.0).astype(jnp.bfloat16),
        "validity": draw_validity(jax.random.fold_in(arg_keys[7], 71), 0),
    }


def reference(features, value_weight, output_weight, hit_list, sample_index, attention, validity):
    values = jnp.dot(features, value_weight, preferred_element_type=jnp.float32).astype(jnp.bfloat16)
    value_heads = values.astype(jnp.float32).reshape(-1, H, D // H)
    hit_count = jnp.sum(validity, axis=1)
    inverse = 1.0 / jnp.maximum(hit_count, 1).astype(jnp.float32)
    weights = attention.astype(jnp.float32).reshape(-1, 1, H, K) * validity.astype(jnp.float32)[:, :, None, None]
    weights = weights * inverse[:, None, None, None]
    cameras = jnp.repeat(hit_list, Q_TILE, axis=0).astype(jnp.int32)
    targets = (cameras[:, :, None] * CAM_ROWS + sample_index).astype(jnp.int32)
    targets = targets.reshape(TILES, Q_TILE, HITS, H, K)
    weights = weights.reshape(TILES, Q_TILE, HITS, H, K)
    head_ids = jnp.arange(H).astype(jnp.int32).reshape(1, 1, H, 1)

    def per_tile(tile_pair):
        tile_targets, tile_weights = tile_pair
        picked = value_heads[tile_targets, head_ids]
        return jnp.sum(tile_weights[..., None] * picked, axis=(1, 3))

    sampled = lax.map(per_tile, (targets, weights)).reshape(TILES * Q_TILE, D)
    attended = sampled.astype(jnp.bfloat16)
    return jnp.dot(attended, output_weight, preferred_element_type=jnp.float32).astype(jnp.bfloat16)
```

```python
import jax
import jax.numpy as jnp
from jax import lax
from jax.experimental import pallas as pl
from jax.experimental.pallas import tpu as pltpu
from jax.sharding import Mesh, PartitionSpec as P

D = 256
H = 8
K = 8
HITS = 2
CAM_ROWS = 1024
Q = 512
CAM_DEVICES = 8

BLOCK = 24
STRIPE = CAM_DEVICES * BLOCK
WINDOW = 3 * BLOCK
CHUNK = 16
LANES = H * CHUNK
CHUNKS = 2 * HITS * WINDOW // CHUNK
Q_STEP = 32

whole = pl.BlockSpec(memory_space=pltpu.VMEM)
scalars = pl.BlockSpec(memory_space=pltpu.SMEM)


def slot_chunks(slot):
    found = []
    for half in range(2):
        first = (half * HITS + slot) * WINDOW
        found += range(first // CHUNK, (first + WINDOW - 1) // CHUNK + 1)
    return found


def mix_kernel(place_ref, hit_ref, index_ref, attention_ref, validity_ref, mix_ref, row_ref, weight_ref):
    core, cam = place_ref[0], place_ref[1]
    hit_count = validity_ref[0:1, :] + validity_ref[1:2, :]
    inverse = 1.0 / jnp.maximum(hit_count, 1).astype(jnp.float32)
    attention = attention_ref[...].astype(jnp.float32)
    rows, weights = [], []
    for slot in range(HITS):
        camera = hit_ref[0, slot]
        stripe = (camera * 16) // 3
        shifted = index_ref[slot] + (camera * CAM_ROWS - stripe * STRIPE)
        step = (shifted * 683) >> 17
        within = shifted - step * STRIPE
        owner = (within * 171) >> 12
        row = within - owner * BLOCK + (step >> 1) * BLOCK
        other = ((step + stripe) & 1) != core
        row = jnp.where(other, row + HITS * WINDOW, row)
        row = jnp.where(owner == cam, row, -2 * CHUNK)
        rows.append(row.astype(jnp.float32))
        weights.append(attention * validity_ref[slot : slot + 1, :].astype(jnp.float32) * inverse)
    rows = jnp.concatenate(rows, axis=0).T.astype(jnp.bfloat16)
    weights = jnp.concatenate(weights, axis=0).T.astype(jnp.bfloat16)
    source = lax.broadcasted_iota(jnp.int32, (HITS * H * K, LANES), 0)
    lane = lax.broadcasted_iota(jnp.int32, (HITS * H * K, LANES), 1)
    for slot in range(HITS):
        for k in range(K):
            spread = (source == slot * H * K + (lane // CHUNK) * K + k).astype(jnp.bfloat16)
            row_ref[slot * K + k] = jnp.dot(rows, spread, preferred_element_type=jnp.float32)
            weight_ref[slot * K + k] = jnp.dot(weights, spread, preferred_element_type=jnp.float32)

    local = lax.broadcasted_iota(jnp.int32, (1, LANES), 1) % CHUNK

    @pl.loop(0, Q // Q_STEP)
    def _(step):
        part = pl.ds(pl.multiple_of(step * Q_STEP, Q_STEP), Q_STEP)
        sums = {}
        for slot in range(HITS):
            picked = [row_ref[slot * K + k, part, :] for k in range(K)]
            scale = [weight_ref[slot * K + k, part, :] for k in range(K)]
            for chunk in slot_chunks(slot):
                target = (local + (chunk * CHUNK - slot * WINDOW)).astype(jnp.float32)
                total = sums.get(chunk)
                if total is None:
                    total = jnp.zeros((Q_STEP, LANES), jnp.float32)
                for k in range(K):
                    total = jnp.where(picked[k] == target, scale[k], total)
                sums[chunk] = total
        for chunk, total in sums.items():
            mix_ref[part, chunk * LANES : (chunk + 1) * LANES] = total.astype(jnp.bfloat16)


def build_mix(place, hit_list, index, attention, validity):
    return pl.pallas_call(
        mix_kernel,
        out_shape=jax.ShapeDtypeStruct((Q, CHUNKS * LANES), jnp.bfloat16),
        in_specs=[scalars, scalars, whole, whole, whole],
        out_specs=whole,
        scratch_shapes=[
            pltpu.VMEM((HITS * K, Q, LANES), jnp.float32),
            pltpu.VMEM((HITS * K, Q, LANES), jnp.float32),
        ],
        compiler_params=pltpu.CompilerParams(vmem_limit_bytes=24 << 20),
        cost_estimate=pl.CostEstimate(flops=1 << 29, bytes_accessed=4 << 20, transcendentals=0),
        name="build_mix",
    )(place, hit_list, index, attention, validity)


def sample_kernel(place_ref, hit_ref, mine_ref, other_ref, weight_ref, mix_ref, out_ref):
    core = place_ref[0]
    windows = []
    for ref, parity in ((mine_ref, core), (other_ref, 1 - core)):
        for slot in range(HITS):
            stripe = (hit_ref[0, slot] * 16) // 3
            first = ((stripe + 1 - parity) // 2) * BLOCK
            windows.append(ref[pl.ds(pl.multiple_of(first, 8), WINDOW), :])
    features = jnp.concatenate(windows, axis=0)
    values = jnp.dot(features, weight_ref[...], preferred_element_type=jnp.float32)
    head_of_row = lax.broadcasted_iota(jnp.int32, (LANES, D), 0) // CHUNK
    head_of_column = lax.broadcasted_iota(jnp.int32, (LANES, D), 1) // (D // H)
    same_head = head_of_row == head_of_column
    total = jnp.zeros((Q, D), jnp.float32)
    for pair in range(CHUNKS // 2):
        blocks = []
        for chunk in (2 * pair, 2 * pair + 1):
            piece = values[chunk * CHUNK : (chunk + 1) * CHUNK, :]
            tall = jnp.concatenate([piece] * H, axis=0)
            blocks.append(jnp.where(same_head, tall, 0.0).astype(jnp.bfloat16))
        block = jnp.concatenate(blocks, axis=0)
        total = total + jnp.dot(
            mix_ref[:, 2 * pair * LANES : (2 * pair + 2) * LANES], block, preferred_element_type=jnp.float32
        )
    out_ref[...] = total.astype(jnp.bfloat16)


def sample(place, hit_list, mine, other, value_weight, mix):
    return pl.pallas_call(
        sample_kernel,
        out_shape=jax.ShapeDtypeStruct((Q, D), jnp.bfloat16),
        in_specs=[scalars, scalars, whole, whole, whole, whole],
        out_specs=whole,
        compiler_params=pltpu.CompilerParams(vmem_limit_bytes=24 << 20),
        cost_estimate=pl.CostEstimate(flops=1 << 29, bytes_accessed=4 << 20, transcendentals=0),
        name="sample",
    )(place, hit_list, mine, other, value_weight, mix)


def project_kernel(pieces_ref, weight_ref, out_ref):
    total = pieces_ref[0].astype(jnp.float32)
    for i in range(1, CAM_DEVICES):
        total = total + pieces_ref[i].astype(jnp.float32)
    out_ref[...] = jnp.dot(
        total.astype(jnp.bfloat16), weight_ref[...], preferred_element_type=jnp.float32
    ).astype(jnp.bfloat16)


def project(pieces, output_weight):
    return pl.pallas_call(
        project_kernel,
        out_shape=jax.ShapeDtypeStruct((Q // CAM_DEVICES, D), jnp.bfloat16),
        in_specs=[whole, whole],
        out_specs=whole,
        name="project",
    )(pieces, output_weight)


def body(features, value_weight, output_weight, hit_list, sample_index, attention, validity):
    place = jnp.stack([lax.axis_index("core"), lax.axis_index("cam")]).astype(jnp.int32)
    copies = jnp.broadcast_to(features[None], (16, BLOCK, D))
    mine = lax.all_to_all(copies, ("z", "y"), 0, 0, tiled=True).reshape(16 * BLOCK, D)
    index = sample_index.transpose(1, 2, 0)
    mix = build_mix(place, hit_list, index, attention.T, validity.T)
    mine, mix = lax.optimization_barrier((mine, mix))
    other = lax.ppermute(mine, "core", [(0, 1), (1, 0)])
    partial_sums = sample(place, hit_list, mine, other, value_weight, mix)
    pieces = partial_sums.reshape(CAM_DEVICES, Q // CAM_DEVICES, D)
    arrived = lax.all_to_all(pieces, "cam", 0, 0, tiled=True)
    return project(arrived, output_weight)


def solution(mesh):
    split = Mesh(mesh.devices.reshape(8, 2, 2, CAM_DEVICES), ("z", "y", "core", "cam"))
    tile = ("z", "y", "core")
    every = tile + ("cam",)
    in_specs = (
        P(every, None),
        P(),
        P(),
        P(tile, None),
        P(tile, None, None),
        P(tile, None),
        P(tile, None),
    )
    return jax.shard_map(body, mesh=split, in_specs=in_specs, out_specs=P(every, None), check_vma=False)
```

```python
import jax
import jax.numpy as jnp
from jax import lax
from jax.experimental import pallas as pl
from jax.experimental.pallas import tpu as pltpu
from jax.sharding import Mesh, PartitionSpec as P

D = 256
H = 8
K = 8
HITS = 2
CAM_ROWS = 1024
Q = 512
CAM_DEVICES = 8
Z_DEVICES = 8

BLOCK = 24
STRIPE = CAM_DEVICES * BLOCK
QUAD = 2 * BLOCK
HALF = 2 * QUAD
CHUNK = 16
LANES = H * CHUNK
SLOT_CHUNKS = HALF // CHUNK
HALF_CHUNKS = HITS * SLOT_CHUNKS
Q_STEP = 32

whole = pl.BlockSpec(memory_space=pltpu.VMEM)
scalars = pl.BlockSpec(memory_space=pltpu.SMEM)
anywhere = pl.BlockSpec(memory_space=pltpu.HBM)


def first_stripe(camera):
    return (camera * 16) // 3


def mix_kernel(
    place_ref, hit_ref, index_any, attention_any, validity_any, mix_ref,
    index_ref, attention_ref, validity_ref, row_ref, weight_ref, sems,
):
    copies = [
        pltpu.make_async_copy(source, target, sems.at[i])
        for i, (source, target) in enumerate(
            ((index_any, index_ref), (attention_any, attention_ref), (validity_any, validity_ref))
        )
    ]
    for copy in copies:
        copy.start()
    for copy in copies:
        copy.wait()
    y, core, cam = place_ref[0], place_ref[1], place_ref[2]
    hit_count = validity_ref[0:1, :] + validity_ref[1:2, :]
    inverse = 1.0 / jnp.maximum(hit_count, 1).astype(jnp.float32)
    attention = attention_ref[...].astype(jnp.float32)
    rows, weights = [], []
    for slot in range(HITS):
        camera = hit_ref[0, slot]
        stripe = first_stripe(camera)
        shifted = index_ref[slot] + (camera * CAM_ROWS - stripe * STRIPE)
        step = (shifted * 683) >> 17
        within = shifted - step * STRIPE
        owner = (within * 171) >> 12
        tile = step + stripe
        row = within - owner * BLOCK + ((tile >> 2) & 1) * BLOCK
        row = jnp.where((tile & 1) != core, row + QUAD, row)
        row = jnp.where(((tile >> 1) & 1) != y, row + HALF, row)
        row = jnp.where(owner == cam, row, -1)
        rows.append(row.astype(jnp.float32))
        weights.append(attention * validity_ref[slot : slot + 1, :].astype(jnp.float32) * inverse)
    rows = jnp.concatenate(rows, axis=0).T.astype(jnp.bfloat16)
    weights = jnp.concatenate(weights, axis=0).T.astype(jnp.bfloat16)
    source = lax.broadcasted_iota(jnp.int32, (HITS * H * K, LANES), 0)
    lane = lax.broadcasted_iota(jnp.int32, (HITS * H * K, LANES), 1)
    for slot in range(HITS):
        for k in range(K):
            spread = (source == slot * H * K + (lane // CHUNK) * K + k).astype(jnp.bfloat16)
            row_ref[slot * K + k] = jnp.dot(rows, spread, preferred_element_type=jnp.float32).astype(jnp.bfloat16)
            weight_ref[slot * K + k] = jnp.dot(weights, spread, preferred_element_type=jnp.float32).astype(jnp.bfloat16)

    local = lax.broadcasted_iota(jnp.int32, (Q_STEP, LANES), 1) % CHUNK

    @pl.loop(0, Q // Q_STEP)
    def _(step):
        part = pl.ds(pl.multiple_of(step * Q_STEP, Q_STEP), Q_STEP)
        for slot in range(HITS):
            picked = [row_ref[slot * K + k, part, :] for k in range(K)]
            scale = [weight_ref[slot * K + k, part, :] for k in range(K)]
            for half in range(2):
                for i in range(SLOT_CHUNKS):
                    target = (local + (half * HALF + i * CHUNK)).astype(jnp.float32).astype(jnp.bfloat16)
                    total = jnp.zeros((Q_STEP, LANES), jnp.bfloat16)
                    for k in range(K):
                        total = jnp.where(picked[k] == target, scale[k], total)
                    chunk = slot * SLOT_CHUNKS + i
                    mix_ref[half, part, chunk * LANES : (chunk + 1) * LANES] = total


def build_mix(place, hit_list, index, attention, validity):
    return pl.pallas_call(
        mix_kernel,
        out_shape=jax.ShapeDtypeStruct((2, Q, HALF_CHUNKS * LANES), jnp.bfloat16),
        in_specs=[scalars, scalars, anywhere, anywhere, anywhere],
        out_specs=whole,
        scratch_shapes=[
            pltpu.VMEM((HITS, H * K, Q), jnp.int32),
            pltpu.VMEM((H * K, Q), jnp.bfloat16),
            pltpu.VMEM((HITS, Q), jnp.int32),
            pltpu.VMEM((HITS * K, Q, LANES), jnp.bfloat16),
            pltpu.VMEM((HITS * K, Q, LANES), jnp.bfloat16),
            pltpu.SemaphoreType.DMA((3,)),
        ],
        compiler_params=pltpu.CompilerParams(vmem_limit_bytes=16 << 20),
        cost_estimate=pl.CostEstimate(flops=1 << 29, bytes_accessed=4 << 20, transcendentals=0),
        name="build_mix",
    )(place, hit_list, index, attention, validity)


def mixed(place_ref, hit_ref, mine_ref, other_ref, weight_ref, mix, y):
    core = place_ref[1]
    blocks = []
    for slot in range(HITS):
        stripe = first_stripe(hit_ref[0, slot])
        for ref, place_core in ((mine_ref, core), (other_ref, 1 - core)):
            place = 2 * y + place_core
            first = (stripe + ((place - stripe) & 3) - place) // 4
            first = jnp.minimum(first, Z_DEVICES - 2)
            for parity in range(2):
                z = first + ((first + parity) & 1)
                blocks.append(ref[pl.ds(pl.multiple_of(z * BLOCK, 8), BLOCK), :])
    features = jnp.concatenate(blocks, axis=0)
    values = jnp.dot(features, weight_ref[...], preferred_element_type=jnp.float32)
    head_of_row = lax.broadcasted_iota(jnp.int32, (LANES, D), 0) // CHUNK
    head_of_column = lax.broadcasted_iota(jnp.int32, (LANES, D), 1) // (D // H)
    same_head = head_of_row == head_of_column
    total = jnp.zeros((Q, D), jnp.float32)
    for pair in range(HALF_CHUNKS // 2):
        blocks = []
        for chunk in (2 * pair, 2 * pair + 1):
            piece = values[chunk * CHUNK : (chunk + 1) * CHUNK, :]
            tall = jnp.concatenate([piece] * H, axis=0)
            blocks.append(jnp.where(same_head, tall, 0.0).astype(jnp.bfloat16))
        block = jnp.concatenate(blocks, axis=0)
        columns = slice(2 * pair * LANES, (2 * pair + 2) * LANES)
        total = total + jnp.dot(mix[:, columns], block, preferred_element_type=jnp.float32)
    return total


def near_kernel(place_ref, hit_ref, mine_ref, other_ref, weight_ref, mix_ref, out_ref):
    out_ref[...] = mixed(place_ref, hit_ref, mine_ref, other_ref, weight_ref, mix_ref.at[0], place_ref[0])


def far_kernel(place_ref, hit_ref, mine_ref, other_ref, weight_ref, mix_ref, near_ref, out_ref):
    total = mixed(place_ref, hit_ref, mine_ref, other_ref, weight_ref, mix_ref.at[1], 1 - place_ref[0])
    out_ref[...] = (near_ref[...] + total).astype(jnp.bfloat16)


def sample(kernel, kind, name, *operands):
    return pl.pallas_call(
        kernel,
        out_shape=jax.ShapeDtypeStruct((Q, D), kind),
        in_specs=[scalars, scalars] + [whole] * (len(operands) - 2),
        out_specs=whole,
        compiler_params=pltpu.CompilerParams(vmem_limit_bytes=16 << 20),
        cost_estimate=pl.CostEstimate(flops=1 << 29, bytes_accessed=2 << 20, transcendentals=0),
        name=name,
    )(*operands)


def project_kernel(pieces_ref, weight_ref, out_ref):
    total = pieces_ref[0].astype(jnp.float32)
    for i in range(1, CAM_DEVICES):
        total = total + pieces_ref[i].astype(jnp.float32)
    out_ref[...] = jnp.dot(
        total.astype(jnp.bfloat16), weight_ref[...], preferred_element_type=jnp.float32
    ).astype(jnp.bfloat16)


def project(pieces, output_weight):
    return pl.pallas_call(
        project_kernel,
        out_shape=jax.ShapeDtypeStruct((Q // CAM_DEVICES, D), jnp.bfloat16),
        in_specs=[whole, whole],
        out_specs=whole,
        compiler_params=pltpu.CompilerParams(vmem_limit_bytes=8 << 20),
        name="project",
    )(pieces, output_weight)


def swapped(x, axis):
    return lax.ppermute(x, axis, [(0, 1), (1, 0)])


def body(features, value_weight, output_weight, hit_list, sample_index, attention, validity):
    place = jnp.stack([lax.axis_index("y"), lax.axis_index("core"), lax.axis_index("cam")]).astype(jnp.int32)
    copies = jnp.broadcast_to(features[None], (Z_DEVICES, BLOCK, D))
    mine = lax.all_to_all(copies, "z", 0, 0, tiled=True).reshape(Z_DEVICES * BLOCK, D)
    mix = build_mix(place, hit_list, sample_index.transpose(1, 2, 0), attention.T, validity.T)
    mine, mix = lax.optimization_barrier((mine, mix))
    far_mine = swapped(mine, "y")
    other = swapped(mine, "core")
    near = sample(near_kernel, jnp.float32, "sample_near", place, hit_list, mine, other, value_weight, mix)
    far_mine, near = lax.optimization_barrier((far_mine, near))
    far_other = swapped(far_mine, "core")
    partial_sums = sample(
        far_kernel, jnp.bfloat16, "sample_far", place, hit_list, far_mine, far_other, value_weight, mix, near
    )
    pieces = partial_sums.reshape(CAM_DEVICES, Q // CAM_DEVICES, D)
    arrived = lax.all_to_all(pieces, "cam", 0, 0, tiled=True)
    return project(arrived, output_weight)


def solution(mesh):
    split = Mesh(mesh.devices.reshape(Z_DEVICES, 2, 2, CAM_DEVICES), ("z", "y", "core", "cam"))
    tile = ("z", "y", "core")
    every = tile + ("cam",)
    in_specs = (
        P(every, None),
        P(),
        P(),
        P(tile, None),
        P(tile, None, None),
        P(tile, None),
        P(tile, None),
    )
    return jax.shard_map(body, mesh=split, in_specs=in_specs, out_specs=P(every, None), check_vma=False)
```

```python
import jax
import jax.numpy as jnp
from jax import lax
from jax.experimental import pallas as pl
from jax.experimental.pallas import tpu as pltpu
from jax.sharding import Mesh, PartitionSpec as P

D = 256
H = 8
K = 8
HITS = 2
CAM_ROWS = 1024
Q = 512
CAM_DEVICES = 8
ZY_DEVICES = 16

BLOCK = 24
STRIPE = CAM_DEVICES * BLOCK
STRIPES = 6
WINDOW = STRIPES * BLOCK
CHUNK = 16
LANES = H * CHUNK
CHUNKS = HITS * WINDOW // CHUNK
Q_STEP = 32

whole = pl.BlockSpec(memory_space=pltpu.VMEM)
scalars = pl.BlockSpec(memory_space=pltpu.SMEM)
anywhere = pl.BlockSpec(memory_space=pltpu.HBM)


def first_stripe(camera):
    return (camera * 16) // 3


def mix_kernel(
    place_ref, hit_any, index_any, attention_any, validity_any, mix_ref,
    hit_ref, index_ref, attention_ref, validity_ref, row_ref, weight_ref, sems,
):
    copies = [
        pltpu.make_async_copy(source, target, sems.at[i])
        for i, (source, target) in enumerate(
            (
                (index_any, index_ref),
                (attention_any, attention_ref),
                (validity_any, validity_ref),
                (hit_any, hit_ref),
            )
        )
    ]
    for copy in copies:
        copy.start()
    for copy in copies:
        copy.wait()
    cam = place_ref[1]
    hit_count = validity_ref[0:1, :] + validity_ref[1:2, :]
    inverse = 1.0 / jnp.maximum(hit_count, 1).astype(jnp.float32)
    attention = attention_ref[...].astype(jnp.float32)
    rows, weights = [], []
    for slot in range(HITS):
        camera = hit_ref[0, slot]
        shifted = index_ref[slot] + (camera * CAM_ROWS - first_stripe(camera) * STRIPE)
        stripe = (shifted * 683) >> 17
        within = shifted - stripe * STRIPE
        owner = (within * 171) >> 12
        row = within - owner * BLOCK + stripe * BLOCK
        row = jnp.where(owner == cam, row, -2 * CHUNK)
        rows.append(row.astype(jnp.float32))
        weights.append(attention * validity_ref[slot : slot + 1, :].astype(jnp.float32) * inverse)
    rows = jnp.concatenate(rows, axis=0).T.astype(jnp.bfloat16)
    weights = jnp.concatenate(weights, axis=0).T.astype(jnp.bfloat16)
    source = lax.broadcasted_iota(jnp.int32, (HITS * H * K, LANES), 0)
    lane = lax.broadcasted_iota(jnp.int32, (HITS * H * K, LANES), 1)
    for slot in range(HITS):
        for k in range(K):
            spread = (source == slot * H * K + (lane // CHUNK) * K + k).astype(jnp.bfloat16)
            spread_rows = jnp.dot(rows, spread, preferred_element_type=jnp.float32)
            row_ref[slot * K + k] = spread_rows.astype(jnp.int32).astype(jnp.int16)
            spread_weights = jnp.dot(weights, spread, preferred_element_type=jnp.float32)
            weight_ref[slot * K + k] = spread_weights.astype(jnp.bfloat16)

    local = lax.broadcasted_iota(jnp.int32, (Q_STEP, LANES), 1) % CHUNK

    @pl.loop(0, Q // Q_STEP)
    def _(step):
        part = pl.ds(pl.multiple_of(step * Q_STEP, Q_STEP), Q_STEP)
        for slot in range(HITS):
            picked = [row_ref[slot * K + k, part, :] for k in range(K)]
            scale = [weight_ref[slot * K + k, part, :] for k in range(K)]
            for chunk in slot_chunks(slot):
                target = (local + (chunk * CHUNK - slot * WINDOW)).astype(jnp.int16)
                total = jnp.zeros((Q_STEP, LANES), jnp.bfloat16)
                for k in range(K):
                    total = jnp.where(picked[k] == target, scale[k], total)
                mix_ref[part, chunk * LANES : (chunk + 1) * LANES] = total


def slot_chunks(slot):
    return range(slot * WINDOW // CHUNK, (slot + 1) * WINDOW // CHUNK)


def build_mix(place, hit_list, index, attention, validity):
    inputs = (pltpu.with_memory_space_constraint(x, pltpu.HBM) for x in (hit_list, index, attention, validity))
    return pl.pallas_call(
        mix_kernel,
        out_shape=jax.ShapeDtypeStruct((Q, CHUNKS * LANES), jnp.bfloat16),
        in_specs=[scalars, anywhere, anywhere, anywhere, anywhere],
        out_specs=whole,
        scratch_shapes=[
            pltpu.SMEM((1, HITS), jnp.int32),
            pltpu.VMEM((HITS, H * K, Q), jnp.int32),
            pltpu.VMEM((H * K, Q), jnp.bfloat16),
            pltpu.VMEM((HITS, Q), jnp.int32),
            pltpu.VMEM((HITS * K, Q, LANES), jnp.int16),
            pltpu.VMEM((HITS * K, Q, LANES), jnp.bfloat16),
            pltpu.SemaphoreType.DMA((4,)),
        ],
        compiler_params=pltpu.CompilerParams(vmem_limit_bytes=16 << 20),
        cost_estimate=pl.CostEstimate(flops=1 << 29, bytes_accessed=4 << 20, transcendentals=0),
        name="build_mix",
    )(place, *inputs)


def sample_kernel(place_ref, hit_ref, mine_ref, other_ref, weight_ref, mix_ref, out_ref):
    core = place_ref[0]
    blocks = []
    for slot in range(HITS):
        first = first_stripe(hit_ref[0, slot])
        for i in range(STRIPES):
            tile = first + i
            part = pl.ds(pl.multiple_of((ZY_DEVICES - 1 - (tile >> 1)) * BLOCK, 8), BLOCK)
            blocks.append(jnp.where((tile & 1) == core, mine_ref[part, :], other_ref[part, :]))
    features = jnp.concatenate(blocks, axis=0)
    values = jnp.dot(features, weight_ref[...], preferred_element_type=jnp.float32)
    head_of_row = lax.broadcasted_iota(jnp.int32, (LANES, D), 0) // CHUNK
    head_of_column = lax.broadcasted_iota(jnp.int32, (LANES, D), 1) // (D // H)
    same_head = head_of_row == head_of_column
    total = jnp.zeros((Q, D), jnp.float32)
    for pair in range(CHUNKS // 2):
        blocks = []
        for chunk in (2 * pair, 2 * pair + 1):
            piece = values[chunk * CHUNK : (chunk + 1) * CHUNK, :]
            tall = jnp.concatenate([piece] * H, axis=0)
            blocks.append(jnp.where(same_head, tall, 0.0).astype(jnp.bfloat16))
        block = jnp.concatenate(blocks, axis=0)
        columns = slice(2 * pair * LANES, (2 * pair + 2) * LANES)
        total = total + jnp.dot(mix_ref[:, columns], block, preferred_element_type=jnp.float32)
    total = total.astype(jnp.bfloat16)
    share = Q // CAM_DEVICES
    for i in range(CAM_DEVICES):
        out_ref[CAM_DEVICES - 1 - i] = total[i * share : (i + 1) * share, :]


def sample(*operands):
    return pl.pallas_call(
        sample_kernel,
        out_shape=jax.ShapeDtypeStruct((CAM_DEVICES, Q // CAM_DEVICES, D), jnp.bfloat16),
        in_specs=[scalars, scalars, whole, whole, whole, whole],
        out_specs=whole,
        compiler_params=pltpu.CompilerParams(vmem_limit_bytes=16 << 20),
        cost_estimate=pl.CostEstimate(flops=1 << 29, bytes_accessed=2 << 20, transcendentals=0),
        name="sample",
    )(*operands)


def project_kernel(pieces_ref, weight_ref, out_ref):
    total = pieces_ref[0].astype(jnp.float32)
    for i in range(1, CAM_DEVICES):
        total = total + pieces_ref[i].astype(jnp.float32)
    out_ref[...] = jnp.dot(
        total.astype(jnp.bfloat16), weight_ref[...], preferred_element_type=jnp.float32
    ).astype(jnp.bfloat16)


def project(pieces, output_weight):
    return pl.pallas_call(
        project_kernel,
        out_shape=jax.ShapeDtypeStruct((Q // CAM_DEVICES, D), jnp.bfloat16),
        in_specs=[whole, whole],
        out_specs=whole,
        compiler_params=pltpu.CompilerParams(vmem_limit_bytes=8 << 20),
        name="project",
    )(pieces, output_weight)


def swapped(x, axis):
    return lax.ppermute(x, axis, [(0, 1), (1, 0)])


def exchanged(x, axis, order):
    return lax.all_to_all(x, axis, 0, 0, tiled=True, axis_index_groups=[order])


def body(features, value_weight, output_weight, hit_list, sample_index, attention, validity):
    place = jnp.stack([lax.axis_index("core"), lax.axis_index("cam")]).astype(jnp.int32)
    copies = jnp.broadcast_to(features[None], (ZY_DEVICES, BLOCK, D))
    mine = exchanged(copies, "zy", list(reversed(range(ZY_DEVICES)))).reshape(ZY_DEVICES * BLOCK, D)
    mix = build_mix(place, hit_list, sample_index.transpose(1, 2, 0), attention.T, validity.T)
    mine, mix = lax.optimization_barrier((mine, mix))
    other = swapped(mine, "core")
    pieces = sample(place, hit_list, mine, other, value_weight, mix)
    arrived = exchanged(pieces, "cam", list(reversed(range(CAM_DEVICES))))
    return project(arrived, output_weight)


def solution(mesh):
    split = Mesh(mesh.devices.reshape(ZY_DEVICES, 2, CAM_DEVICES), ("zy", "core", "cam"))
    tile = ("zy", "core")
    every = tile + ("cam",)
    in_specs = (
        P(every, None),
        P(),
        P(),
        P(tile, None),
        P(tile, None, None),
        P(tile, None),
        P(tile, None),
    )
    return jax.shard_map(body, mesh=split, in_specs=in_specs, out_specs=P(every, None), check_vma=False)
```

```python
import jax
import jax.numpy as jnp
from jax import lax
from jax.experimental import pallas as pl
from jax.experimental.pallas import tpu as pltpu
from jax.sharding import Mesh, PartitionSpec as P

D = 256
H = 8
K = 8
HITS = 2
CAM_ROWS = 1024
Q = 512
CAM_DEVICES = 8
ZY_DEVICES = 16

BLOCK = 24
STRIPE = CAM_DEVICES * BLOCK
STRIPES = 6
WINDOW = STRIPES * BLOCK
HALF_WINDOW = WINDOW // 2
CHUNK = 16
LANES = H * CHUNK
CHUNKS = HITS * WINDOW // CHUNK
HALF_CHUNKS = CHUNKS // 2
Q_STEP = 32

whole = pl.BlockSpec(memory_space=pltpu.VMEM)
scalars = pl.BlockSpec(memory_space=pltpu.SMEM)
anywhere = pl.BlockSpec(memory_space=pltpu.HBM)


def first_stripe(camera):
    return (camera * 16) // 3


def mix_kernel(
    place_ref, hit_any, index_any, attention_any, validity_any, mix_ref, starts_ref,
    hit_ref, index_ref, attention_ref, validity_ref, row_ref, weight_ref, sems,
):
    copies = [
        pltpu.make_async_copy(source, target, sems.at[i])
        for i, (source, target) in enumerate(
            (
                (index_any, index_ref),
                (attention_any, attention_ref),
                (validity_any, validity_ref),
                (hit_any, hit_ref),
            )
        )
    ]
    for copy in copies:
        copy.start()
    for copy in copies:
        copy.wait()
    core, cam = place_ref[0], place_ref[1]
    hit_count = validity_ref[0:1, :] + validity_ref[1:2, :]
    inverse = 1.0 / jnp.maximum(hit_count, 1).astype(jnp.float32)
    attention = attention_ref[...].astype(jnp.float32)
    rows, weights = [], []
    for slot in range(HITS):
        camera = hit_ref[0, slot]
        shifted = index_ref[slot] + (camera * CAM_ROWS - first_stripe(camera) * STRIPE)
        stripe = (shifted * 683) >> 17
        within = shifted - stripe * STRIPE
        owner = (within * 171) >> 12
        row = within - owner * BLOCK + (STRIPES // 2 - 1 - (stripe >> 1)) * BLOCK
        other = ((stripe + first_stripe(camera)) & 1) != core
        row = jnp.where(other, row + HITS * HALF_WINDOW, row)
        row = jnp.where(owner == cam, row, -2 * CHUNK)
        rows.append(row.astype(jnp.float32))
        weights.append(attention * validity_ref[slot : slot + 1, :].astype(jnp.float32) * inverse)
    rows = jnp.concatenate(rows, axis=0).T.astype(jnp.bfloat16)
    weights = jnp.concatenate(weights, axis=0).T.astype(jnp.bfloat16)
    source = lax.broadcasted_iota(jnp.int32, (HITS * H * K, LANES), 0)
    lane = lax.broadcasted_iota(jnp.int32, (HITS * H * K, LANES), 1)
    for slot in range(HITS):
        for k in range(K):
            spread = (source == slot * H * K + (lane // CHUNK) * K + k).astype(jnp.bfloat16)
            spread_rows = jnp.dot(rows, spread, preferred_element_type=jnp.float32)
            row_ref[slot * K + k] = spread_rows.astype(jnp.int32).astype(jnp.int16)
            spread_weights = jnp.dot(weights, spread, preferred_element_type=jnp.float32)
            weight_ref[slot * K + k] = spread_weights.astype(jnp.bfloat16)

    for half, parity in enumerate((core, 1 - core)):
        for slot in range(HITS):
            last = (first_stripe(hit_ref[0, slot]) + 1 - parity) // 2 + STRIPES // 2 - 1
            line = half * HITS + slot
            starts_ref[line : line + 1, :] = jnp.full((1, LANES), (ZY_DEVICES - 1 - last) * BLOCK, jnp.int32)

    local = lax.broadcasted_iota(jnp.int32, (Q_STEP, LANES), 1) % CHUNK

    @pl.loop(0, Q // Q_STEP)
    def _(step):
        part = pl.ds(pl.multiple_of(step * Q_STEP, Q_STEP), Q_STEP)
        sums = {}
        for slot in range(HITS):
            picked = [row_ref[slot * K + k, part, :] for k in range(K)]
            scale = [weight_ref[slot * K + k, part, :] for k in range(K)]
            for chunk in slot_chunks(slot):
                target = (local + (chunk * CHUNK - slot * HALF_WINDOW)).astype(jnp.int16)
                total = sums.pop(chunk, None)
                if total is None:
                    total = jnp.zeros((Q_STEP, LANES), jnp.bfloat16)
                for k in range(K):
                    total = jnp.where(picked[k] == target, scale[k], total)
                if slot == 0 and chunk in slot_chunks(1):
                    sums[chunk] = total
                else:
                    mix_ref[part, chunk * LANES : (chunk + 1) * LANES] = total


def slot_chunks(slot):
    found = []
    for half in range(2):
        first = (half * HITS + slot) * HALF_WINDOW
        found += range(first // CHUNK, (first + HALF_WINDOW - 1) // CHUNK + 1)
    return found


def build_mix(place, hit_list, index, attention, validity):
    inputs = (pltpu.with_memory_space_constraint(x, pltpu.HBM) for x in (hit_list, index, attention, validity))
    return pl.pallas_call(
        mix_kernel,
        out_shape=(
            jax.ShapeDtypeStruct((Q, CHUNKS * LANES), jnp.bfloat16),
            jax.ShapeDtypeStruct((2 * HITS, LANES), jnp.int32),
        ),
        in_specs=[scalars, anywhere, anywhere, anywhere, anywhere],
        out_specs=(whole, whole),
        scratch_shapes=[
            pltpu.SMEM((1, HITS), jnp.int32),
            pltpu.VMEM((HITS, H * K, Q), jnp.int32),
            pltpu.VMEM((H * K, Q), jnp.bfloat16),
            pltpu.VMEM((HITS, Q), jnp.int32),
            pltpu.VMEM((HITS * K, Q, LANES), jnp.int16),
            pltpu.VMEM((HITS * K, Q, LANES), jnp.bfloat16),
            pltpu.SemaphoreType.DMA((4,)),
        ],
        compiler_params=pltpu.CompilerParams(vmem_limit_bytes=16 << 20),
        cost_estimate=pl.CostEstimate(flops=1 << 29, bytes_accessed=4 << 20, transcendentals=0),
        name="build_mix",
    )(place, *inputs)


def mixed(starts_ref, gathered_ref, half, weight_ref, mix, spread_ref):
    windows = []
    for slot in range(HITS):
        start = pl.multiple_of(starts_ref[half * HITS + slot, 0], 8)
        windows.append(gathered_ref[pl.ds(start, HALF_WINDOW), :])
    features = jnp.concatenate(windows, axis=0)
    values = jnp.dot(features, weight_ref[...], preferred_element_type=jnp.float32).astype(jnp.bfloat16)
    head_of_row = lax.broadcasted_iota(jnp.int32, (LANES, D), 0) // CHUNK
    head_of_column = lax.broadcasted_iota(jnp.int32, (LANES, D), 1) // (D // H)
    same_head = head_of_row == head_of_column
    for chunk in range(HALF_CHUNKS):
        piece = values[chunk * CHUNK : (chunk + 1) * CHUNK, :]
        tall = jnp.concatenate([piece] * H, axis=0)
        spread_ref[chunk * LANES : (chunk + 1) * LANES, :] = jnp.where(same_head, tall, jnp.zeros((), jnp.bfloat16))
    return jnp.dot(mix, spread_ref[...], preferred_element_type=jnp.float32)


def near_kernel(starts_ref, mine_ref, weight_ref, mix_ref, out_ref, spread_ref):
    out_ref[...] = mixed(starts_ref, mine_ref, 0, weight_ref, mix_ref[:, : HALF_CHUNKS * LANES], spread_ref)


def far_kernel(starts_ref, other_ref, weight_ref, mix_ref, near_ref, out_ref, spread_ref):
    total = near_ref[...] + mixed(
        starts_ref, other_ref, 1, weight_ref, mix_ref[:, HALF_CHUNKS * LANES :], spread_ref
    )
    total = total.astype(jnp.bfloat16)
    share = Q // CAM_DEVICES
    for i in range(CAM_DEVICES):
        out_ref[CAM_DEVICES - 1 - i] = total[i * share : (i + 1) * share, :]


def sample(kernel, name, out_shape, *operands):
    return pl.pallas_call(
        kernel,
        out_shape=out_shape,
        in_specs=[whole] * len(operands),
        out_specs=whole,
        scratch_shapes=[pltpu.VMEM((HALF_CHUNKS * LANES, D), jnp.bfloat16)],
        compiler_params=pltpu.CompilerParams(vmem_limit_bytes=16 << 20),
        cost_estimate=pl.CostEstimate(flops=1 << 28, bytes_accessed=1 << 20, transcendentals=0),
        name=name,
    )(*operands)


def project_kernel(pieces_ref, weight_ref, out_ref):
    total = pieces_ref[0].astype(jnp.float32)
    for i in range(1, CAM_DEVICES):
        total = total + pieces_ref[i].astype(jnp.float32)
    out_ref[...] = jnp.dot(
        total.astype(jnp.bfloat16), weight_ref[...], preferred_element_type=jnp.float32
    ).astype(jnp.bfloat16)


def project(pieces, output_weight):
    return pl.pallas_call(
        project_kernel,
        out_shape=jax.ShapeDtypeStruct((Q // CAM_DEVICES, D), jnp.bfloat16),
        in_specs=[whole, whole],
        out_specs=whole,
        compiler_params=pltpu.CompilerParams(vmem_limit_bytes=8 << 20),
        name="project",
    )(pieces, output_weight)


def swapped(x, axis):
    return lax.ppermute(x, axis, [(0, 1), (1, 0)])


def exchanged(x, axis, order):
    return lax.all_to_all(x, axis, 0, 0, tiled=True, axis_index_groups=[order])


def body(features, value_weight, output_weight, hit_list, sample_index, attention, validity):
    place = jnp.stack([lax.axis_index("core"), lax.axis_index("cam")]).astype(jnp.int32)
    copies = jnp.broadcast_to(features[None], (ZY_DEVICES, BLOCK, D))
    mine = exchanged(copies, "zy", list(reversed(range(ZY_DEVICES)))).reshape(ZY_DEVICES * BLOCK, D)
    mix, starts = build_mix(place, hit_list, sample_index.transpose(1, 2, 0), attention.T, validity.T)
    mine, mix, starts = lax.optimization_barrier((mine, mix, starts))
    other = swapped(mine, "core")
    near_shape = jax.ShapeDtypeStruct((Q, D), jnp.float32)
    near = sample(near_kernel, "sample_near", near_shape, starts, mine, value_weight, mix)
    pieces_shape = jax.ShapeDtypeStruct((CAM_DEVICES, Q // CAM_DEVICES, D), jnp.bfloat16)
    pieces = sample(far_kernel, "sample_far", pieces_shape, starts, other, value_weight, mix, near)
    arrived = exchanged(pieces, "cam", list(reversed(range(CAM_DEVICES))))
    return project(arrived, output_weight)


def solution(mesh):
    split = Mesh(mesh.devices.reshape(ZY_DEVICES, 2, CAM_DEVICES), ("zy", "core", "cam"))
    tile = ("zy", "core")
    every = tile + ("cam",)
    in_specs = (
        P(every, None),
        P(),
        P(),
        P(tile, None),
        P(tile, None, None),
        P(tile, None),
        P(tile, None),
    )
    return jax.shard_map(body, mesh=split, in_specs=in_specs, out_specs=P(every, None), check_vma=False)
```

```python
import jax
import jax.numpy as jnp
from jax import lax
from jax.experimental import pallas as pl
from jax.experimental.pallas import tpu as pltpu
from jax.sharding import Mesh, PartitionSpec as P

D = 256
H = 8
K = 8
HITS = 2
CAM_ROWS = 1024
Q = 512
CAM_DEVICES = 8
ZY_DEVICES = 16

BLOCK = 24
STRIPE = CAM_DEVICES * BLOCK
STRIPES = 6
WINDOW = STRIPES * BLOCK
HALF_WINDOW = WINDOW // 2
CHUNK = 8
LANES = HITS * H * CHUNK
CHUNKS = WINDOW // CHUNK
HALF_CHUNKS = CHUNKS // 2
Q_STEP = 32

whole = pl.BlockSpec(memory_space=pltpu.VMEM)
anywhere = pl.BlockSpec(memory_space=pltpu.HBM)


def listed(i):
    return i ^ 9


def first_stripe(camera):
    return (camera * 16) // 3


def mix_kernel(
    hit_any, index_any, attention_any, validity_any, mix_ref, starts_ref,
    hit_ref, index_ref, attention_ref, validity_ref, row_ref, weight_ref, sems,
):
    copies = [
        pltpu.make_async_copy(source, target, sems.at[i])
        for i, (source, target) in enumerate(
            (
                (index_any, index_ref),
                (attention_any, attention_ref),
                (validity_any, validity_ref),
                (hit_any, hit_ref),
            )
        )
    ]
    for copy in copies:
        copy.start()
    for copy in copies:
        copy.wait()
    core, cam = lax.axis_index("core"), lax.axis_index("cam")
    hit_count = validity_ref[0:1, :] + validity_ref[1:2, :]
    inverse = 1.0 / jnp.maximum(hit_count, 1).astype(jnp.float32)
    attention = attention_ref[...].astype(jnp.float32)
    rows, weights = [], []
    for slot in range(HITS):
        camera = hit_ref[0, slot]
        shifted = index_ref[slot] + (camera * CAM_ROWS - first_stripe(camera) * STRIPE)
        stripe = (shifted * 683) >> 17
        within = shifted - stripe * STRIPE
        owner = (within * 171) >> 12
        row = within - owner * BLOCK + (stripe >> 1) * BLOCK
        other = ((stripe + first_stripe(camera)) & 1) != core
        row = jnp.where(other, row + HALF_WINDOW, row)
        row = jnp.where(owner == cam, row, -1)
        rows.append(row.astype(jnp.float32))
        weights.append(attention * validity_ref[slot : slot + 1, :].astype(jnp.float32) * inverse)
    rows = jnp.concatenate(rows, axis=0).T.astype(jnp.bfloat16)
    weights = jnp.concatenate(weights, axis=0).T.astype(jnp.bfloat16)
    source = lax.broadcasted_iota(jnp.int32, (HITS * H * K, LANES), 0)
    group = lax.broadcasted_iota(jnp.int32, (HITS * H * K, LANES), 1) // CHUNK
    for k in range(K):
        spread = (source == group * K + k).astype(jnp.bfloat16)
        spread_rows = jnp.dot(rows, spread, preferred_element_type=jnp.float32)
        row_ref[k] = spread_rows.astype(jnp.int32).astype(jnp.int16)
        spread_weights = jnp.dot(weights, spread, preferred_element_type=jnp.float32)
        weight_ref[k] = spread_weights.astype(jnp.bfloat16)

    for half, parity in enumerate((core, 1 - core)):
        for slot in range(HITS):
            first = (first_stripe(hit_ref[0, slot]) + 1 - parity) // 2
            for i in range(STRIPES // 2):
                line = (half * HITS + slot) * (STRIPES // 2) + i
                starts_ref[line : line + 1, :] = jnp.full((1, LANES), listed(first + i) * BLOCK, jnp.int32)

    local = lax.broadcasted_iota(jnp.int32, (Q_STEP, LANES), 1) % CHUNK

    @pl.loop(0, Q // Q_STEP)
    def _(step):
        part = pl.ds(pl.multiple_of(step * Q_STEP, Q_STEP), Q_STEP)
        picked = [row_ref[k, part, :] for k in range(K)]
        scale = [weight_ref[k, part, :] for k in range(K)]
        for chunk in range(CHUNKS):
            target = (local + chunk * CHUNK).astype(jnp.int16)
            total = jnp.zeros((Q_STEP, LANES), jnp.bfloat16)
            for k in range(K):
                total = jnp.where(picked[k] == target, scale[k], total)
            mix_ref[part, chunk * LANES : (chunk + 1) * LANES] = total.astype(jnp.bfloat16)


def build_mix(hit_list, index, attention, validity):
    inputs = (pltpu.with_memory_space_constraint(x, pltpu.HBM) for x in (hit_list, index, attention, validity))
    return pl.pallas_call(
        mix_kernel,
        out_shape=(
            jax.ShapeDtypeStruct((Q, CHUNKS * LANES), jnp.bfloat16),
            jax.ShapeDtypeStruct((HITS * STRIPES, LANES), jnp.int32),
        ),
        in_specs=[anywhere, anywhere, anywhere, anywhere],
        out_specs=(whole, whole),
        scratch_shapes=[
            pltpu.SMEM((1, HITS), jnp.int32),
            pltpu.VMEM((HITS, H * K, Q), jnp.int32),
            pltpu.VMEM((H * K, Q), jnp.bfloat16),
            pltpu.VMEM((HITS, Q), jnp.int32),
            pltpu.VMEM((K, Q, LANES), jnp.int16),
            pltpu.VMEM((K, Q, LANES), jnp.bfloat16),
            pltpu.SemaphoreType.DMA((4,)),
        ],
        compiler_params=pltpu.CompilerParams(vmem_limit_bytes=16 << 20),
        cost_estimate=pl.CostEstimate(flops=1 << 29, bytes_accessed=4 << 20, transcendentals=0),
        name="build_mix",
    )(*inputs)


def mixed(starts_ref, gathered_ref, half, weight_ref, mix, spread_ref):
    windows = []
    for slot in range(HITS):
        for i in range(STRIPES // 2):
            start = pl.multiple_of(starts_ref[(half * HITS + slot) * (STRIPES // 2) + i, 0], 8)
            windows.append(gathered_ref[pl.ds(start, BLOCK), :])
    features = jnp.concatenate(windows, axis=0)
    values = jnp.dot(features, weight_ref[...], preferred_element_type=jnp.float32)
    head_of_row = (lax.broadcasted_iota(jnp.int32, (LANES, D), 0) // CHUNK) % H
    head_of_column = lax.broadcasted_iota(jnp.int32, (LANES, D), 1) // (D // H)
    same_head = head_of_row == head_of_column
    for chunk in range(HALF_CHUNKS):
        pieces = []
        for slot in range(HITS):
            first = slot * HALF_WINDOW + chunk * CHUNK
            pieces += [values[first : first + CHUNK, :]] * H
        tall = jnp.where(same_head, jnp.concatenate(pieces, axis=0), 0.0)
        spread_ref[chunk * LANES : (chunk + 1) * LANES, :] = tall.astype(jnp.bfloat16)
    return jnp.dot(mix, spread_ref[...], preferred_element_type=jnp.float32)


def near_kernel(starts_ref, mine_ref, weight_ref, mix_ref, out_ref, spread_ref):
    out_ref[...] = mixed(starts_ref, mine_ref, 0, weight_ref, mix_ref[:, : HALF_CHUNKS * LANES], spread_ref)


def far_kernel(starts_ref, other_ref, weight_ref, mix_ref, near_ref, out_ref, spread_ref):
    total = near_ref[...] + mixed(
        starts_ref, other_ref, 1, weight_ref, mix_ref[:, HALF_CHUNKS * LANES :], spread_ref
    )
    total = total.astype(jnp.bfloat16)
    share = Q // CAM_DEVICES
    for i in range(CAM_DEVICES):
        out_ref[CAM_DEVICES - 1 - i] = total[i * share : (i + 1) * share, :]


def sample(kernel, name, out_shape, *operands):
    return pl.pallas_call(
        kernel,
        out_shape=out_shape,
        in_specs=[whole] * len(operands),
        out_specs=whole,
        scratch_shapes=[pltpu.VMEM((HALF_CHUNKS * LANES, D), jnp.bfloat16)],
        compiler_params=pltpu.CompilerParams(vmem_limit_bytes=16 << 20),
        cost_estimate=pl.CostEstimate(flops=1 << 28, bytes_accessed=1 << 20, transcendentals=0),
        name=name,
    )(*operands)


def project_kernel(pieces_ref, weight_ref, out_ref):
    total = pieces_ref[0].astype(jnp.float32)
    for i in range(1, CAM_DEVICES):
        total = total + pieces_ref[i].astype(jnp.float32)
    out_ref[...] = jnp.dot(
        total.astype(jnp.bfloat16), weight_ref[...], preferred_element_type=jnp.float32
    ).astype(jnp.bfloat16)


def project(pieces, output_weight):
    return pl.pallas_call(
        project_kernel,
        out_shape=jax.ShapeDtypeStruct((Q // CAM_DEVICES, D), jnp.bfloat16),
        in_specs=[whole, whole],
        out_specs=whole,
        compiler_params=pltpu.CompilerParams(vmem_limit_bytes=8 << 20),
        name="project",
    )(pieces, output_weight)


def swapped(x, axis):
    return lax.ppermute(x, axis, [(0, 1), (1, 0)])


def exchanged(x, axis, order):
    return lax.all_to_all(x, axis, 0, 0, tiled=True, axis_index_groups=[order])


def body(features, value_weight, output_weight, hit_list, sample_index, attention, validity):
    copies = jnp.broadcast_to(features[None], (ZY_DEVICES, BLOCK, D))
    mine = exchanged(copies, "zy", [listed(i) for i in range(ZY_DEVICES)]).reshape(ZY_DEVICES * BLOCK, D)
    mix, starts = build_mix(hit_list, sample_index.transpose(1, 2, 0), attention.T, validity.T)
    mine, mix, starts = lax.optimization_barrier((mine, mix, starts))
    other = swapped(mine, "core")
    near_shape = jax.ShapeDtypeStruct((Q, D), jnp.float32)
    near = sample(near_kernel, "sample_near", near_shape, starts, mine, value_weight, mix)
    pieces_shape = jax.ShapeDtypeStruct((CAM_DEVICES, Q // CAM_DEVICES, D), jnp.bfloat16)
    pieces = sample(far_kernel, "sample_far", pieces_shape, starts, other, value_weight, mix, near)
    arrived = exchanged(pieces, "cam", list(reversed(range(CAM_DEVICES))))
    return project(arrived, output_weight)


def solution(mesh):
    split = Mesh(mesh.devices.reshape(ZY_DEVICES, 2, CAM_DEVICES), ("zy", "core", "cam"))
    tile = ("zy", "core")
    every = tile + ("cam",)
    in_specs = (
        P(every, None),
        P(),
        P(),
        P(tile, None),
        P(tile, None, None),
        P(tile, None),
        P(tile, None),
    )
    return jax.shard_map(body, mesh=split, in_specs=in_specs, out_specs=P(every, None), check_vma=False)
```

```python
import jax
import jax.numpy as jnp
from jax import lax
from jax.experimental import pallas as pl
from jax.experimental.pallas import tpu as pltpu
from jax.sharding import Mesh, PartitionSpec as P

D = 256
H = 8
K = 8
HITS = 2
CAM_ROWS = 1024
Q = 512
CAM_DEVICES = 8
ZY_DEVICES = 16

BLOCK = 24
STRIPE = CAM_DEVICES * BLOCK
STRIPES = 6
WINDOW = STRIPES * BLOCK
HALF_WINDOW = WINDOW // 2
CHUNK = 8
LANES = HITS * H * CHUNK
CHUNKS = WINDOW // CHUNK
HALF_CHUNKS = CHUNKS // 2
Q_STEP = 32

whole = pl.BlockSpec(memory_space=pltpu.VMEM)
anywhere = pl.BlockSpec(memory_space=pltpu.HBM)


def listed(i):
    return i ^ 9


def cam_listed(i, core):
    return i ^ (7 - core)


def first_stripe(camera):
    return (camera * 16) // 3


def mix_kernel(
    hit_any, index_any, attention_any, validity_any, mix_ref, starts_ref,
    hit_ref, index_ref, attention_ref, validity_ref, row_ref, weight_ref, sems,
):
    copies = [
        pltpu.make_async_copy(source, target, sems.at[i])
        for i, (source, target) in enumerate(
            (
                (index_any, index_ref),
                (attention_any, attention_ref),
                (validity_any, validity_ref),
                (hit_any, hit_ref),
            )
        )
    ]
    for copy in copies:
        copy.start()
    for copy in copies:
        copy.wait()
    core, cam = lax.axis_index("core"), lax.axis_index("cam")
    hit_count = validity_ref[0:1, :] + validity_ref[1:2, :]
    inverse = 1.0 / jnp.maximum(hit_count, 1).astype(jnp.float32)
    attention = attention_ref[...].astype(jnp.float32)
    rows, weights = [], []
    for slot in range(HITS):
        camera = hit_ref[0, slot]
        shifted = index_ref[slot] + (camera * CAM_ROWS - first_stripe(camera) * STRIPE)
        stripe = (shifted * 683) >> 17
        within = shifted - stripe * STRIPE
        owner = (within * 171) >> 12
        row = within - owner * BLOCK + (stripe >> 1) * BLOCK
        other = ((stripe + first_stripe(camera)) & 1) != core
        row = jnp.where(other, row + HALF_WINDOW, row)
        row = jnp.where(owner == cam, row, -1)
        rows.append(row.astype(jnp.float32))
        weights.append(attention * validity_ref[slot : slot + 1, :].astype(jnp.float32) * inverse)
    rows = jnp.concatenate(rows, axis=0).T.astype(jnp.bfloat16)
    weights = jnp.concatenate(weights, axis=0).T.astype(jnp.bfloat16)
    source = lax.broadcasted_iota(jnp.int32, (HITS * H * K, LANES), 0)
    group = lax.broadcasted_iota(jnp.int32, (HITS * H * K, LANES), 1) // CHUNK
    for k in range(K):
        spread = (source == group * K + k).astype(jnp.bfloat16)
        spread_rows = jnp.dot(rows, spread, preferred_element_type=jnp.float32)
        row_ref[k] = spread_rows.astype(jnp.int32).astype(jnp.int16)
        spread_weights = jnp.dot(weights, spread, preferred_element_type=jnp.float32)
        weight_ref[k] = spread_weights.astype(jnp.bfloat16)

    for half, parity in enumerate((core, 1 - core)):
        for slot in range(HITS):
            first = (first_stripe(hit_ref[0, slot]) + 1 - parity) // 2
            for i in range(STRIPES // 2):
                line = (half * HITS + slot) * (STRIPES // 2) + i
                starts_ref[line : line + 1, :] = jnp.full((1, LANES), listed(first + i) * BLOCK, jnp.int32)

    local = lax.broadcasted_iota(jnp.int32, (Q_STEP, LANES), 1) % CHUNK

    @pl.loop(0, Q // Q_STEP)
    def _(step):
        part = pl.ds(pl.multiple_of(step * Q_STEP, Q_STEP), Q_STEP)
        picked = [row_ref[k, part, :] for k in range(K)]
        scale = [weight_ref[k, part, :] for k in range(K)]
        for chunk in range(CHUNKS):
            target = (local + chunk * CHUNK).astype(jnp.int16)
            total = jnp.zeros((Q_STEP, LANES), jnp.bfloat16)
            for k in range(K):
                total = jnp.where(picked[k] == target, scale[k], total)
            mix_ref[part, chunk * LANES : (chunk + 1) * LANES] = total.astype(jnp.bfloat16)


def build_mix(hit_list, index, attention, validity):
    inputs = (pltpu.with_memory_space_constraint(x, pltpu.HBM) for x in (hit_list, index, attention, validity))
    return pl.pallas_call(
        mix_kernel,
        out_shape=(
            jax.ShapeDtypeStruct((Q, CHUNKS * LANES), jnp.bfloat16),
            jax.ShapeDtypeStruct((HITS * STRIPES, LANES), jnp.int32),
        ),
        in_specs=[anywhere, anywhere, anywhere, anywhere],
        out_specs=(whole, whole),
        scratch_shapes=[
            pltpu.SMEM((1, HITS), jnp.int32),
            pltpu.VMEM((HITS, H * K, Q), jnp.int32),
            pltpu.VMEM((H * K, Q), jnp.bfloat16),
            pltpu.VMEM((HITS, Q), jnp.int32),
            pltpu.VMEM((K, Q, LANES), jnp.int16),
            pltpu.VMEM((K, Q, LANES), jnp.bfloat16),
            pltpu.SemaphoreType.DMA((4,)),
        ],
        compiler_params=pltpu.CompilerParams(vmem_limit_bytes=16 << 20),
        cost_estimate=pl.CostEstimate(flops=1 << 29, bytes_accessed=4 << 20, transcendentals=0),
        name="build_mix",
    )(*inputs)


def mixed(starts_ref, gathered_ref, half, weight_ref, mix, spread_ref):
    windows = []
    for slot in range(HITS):
        for i in range(STRIPES // 2):
            start = pl.multiple_of(starts_ref[(half * HITS + slot) * (STRIPES // 2) + i, 0], 8)
            windows.append(gathered_ref[pl.ds(start, BLOCK), :])
    features = jnp.concatenate(windows, axis=0)
    values = jnp.dot(features, weight_ref[...], preferred_element_type=jnp.float32)
    head_of_row = (lax.broadcasted_iota(jnp.int32, (LANES, D), 0) // CHUNK) % H
    head_of_column = lax.broadcasted_iota(jnp.int32, (LANES, D), 1) // (D // H)
    same_head = head_of_row == head_of_column
    for chunk in range(HALF_CHUNKS):
        pieces = []
        for slot in range(HITS):
            first = slot * HALF_WINDOW + chunk * CHUNK
            pieces += [values[first : first + CHUNK, :]] * H
        tall = jnp.where(same_head, jnp.concatenate(pieces, axis=0), 0.0)
        spread_ref[chunk * LANES : (chunk + 1) * LANES, :] = tall.astype(jnp.bfloat16)
    return jnp.dot(mix, spread_ref[...], preferred_element_type=jnp.float32)


def near_kernel(starts_ref, mine_ref, weight_ref, mix_ref, out_ref, spread_ref):
    out_ref[...] = mixed(starts_ref, mine_ref, 0, weight_ref, mix_ref[:, : HALF_CHUNKS * LANES], spread_ref)


def far_kernel(starts_ref, other_ref, weight_ref, mix_ref, near_ref, out_ref, spread_ref):
    total = near_ref[...] + mixed(
        starts_ref, other_ref, 1, weight_ref, mix_ref[:, HALF_CHUNKS * LANES :], spread_ref
    )
    total = total.astype(jnp.bfloat16)
    share = Q // CAM_DEVICES
    core = lax.axis_index("core")
    for i in range(CAM_DEVICES):
        out_ref[cam_listed(i, core)] = total[i * share : (i + 1) * share, :]


def sample(kernel, name, out_shape, *operands):
    return pl.pallas_call(
        kernel,
        out_shape=out_shape,
        in_specs=[whole] * len(operands),
        out_specs=whole,
        scratch_shapes=[pltpu.VMEM((HALF_CHUNKS * LANES, D), jnp.bfloat16)],
        compiler_params=pltpu.CompilerParams(vmem_limit_bytes=16 << 20),
        cost_estimate=pl.CostEstimate(flops=1 << 28, bytes_accessed=1 << 20, transcendentals=0),
        name=name,
    )(*operands)


def project_kernel(pieces_ref, weight_ref, out_ref):
    total = pieces_ref[0].astype(jnp.float32)
    for i in range(1, CAM_DEVICES):
        total = total + pieces_ref[i].astype(jnp.float32)
    out_ref[...] = jnp.dot(
        total.astype(jnp.bfloat16), weight_ref[...], preferred_element_type=jnp.float32
    ).astype(jnp.bfloat16)


def project(pieces, output_weight):
    return pl.pallas_call(
        project_kernel,
        out_shape=jax.ShapeDtypeStruct((Q // CAM_DEVICES, D), jnp.bfloat16),
        in_specs=[whole, whole],
        out_specs=whole,
        compiler_params=pltpu.CompilerParams(vmem_limit_bytes=8 << 20),
        name="project",
    )(pieces, output_weight)


def swapped(x, axis):
    return lax.ppermute(x, axis, [(0, 1), (1, 0)])


def body(features, value_weight, output_weight, hit_list, sample_index, attention, validity):
    copies = jnp.broadcast_to(features[None], (ZY_DEVICES, BLOCK, D))
    mine = lax.all_to_all(
        copies, "zy", 0, 0, tiled=True, axis_index_groups=[[listed(i) for i in range(ZY_DEVICES)]]
    ).reshape(ZY_DEVICES * BLOCK, D)
    mix, starts = build_mix(hit_list, sample_index.transpose(1, 2, 0), attention.T, validity.T)
    mine, mix, starts = lax.optimization_barrier((mine, mix, starts))
    other = swapped(mine, "core")
    near_shape = jax.ShapeDtypeStruct((Q, D), jnp.float32)
    near = sample(near_kernel, "sample_near", near_shape, starts, mine, value_weight, mix)
    pieces_shape = jax.ShapeDtypeStruct((CAM_DEVICES, Q // CAM_DEVICES, D), jnp.bfloat16)
    pieces = sample(far_kernel, "sample_far", pieces_shape, starts, other, value_weight, mix, near)
    groups = [
        [(zy * 2 + core) * CAM_DEVICES + cam_listed(i, core) for i in range(CAM_DEVICES)]
        for zy in range(ZY_DEVICES)
        for core in range(2)
    ]
    arrived = lax.all_to_all(pieces, ("zy", "core", "cam"), 0, 0, tiled=True, axis_index_groups=groups)
    return project(arrived, output_weight)


def solution(mesh):
    split = Mesh(mesh.devices.reshape(ZY_DEVICES, 2, CAM_DEVICES), ("zy", "core", "cam"))
    tile = ("zy", "core")
    every = tile + ("cam",)
    in_specs = (
        P(every, None),
        P(),
        P(),
        P(tile, None),
        P(tile, None, None),
        P(tile, None),
        P(tile, None),
    )
    return jax.shard_map(body, mesh=split, in_specs=in_specs, out_specs=P(every, None), check_vma=False)
```

```python
import jax
import jax.numpy as jnp
from jax import lax
from jax.experimental import pallas as pl
from jax.experimental.pallas import tpu as pltpu
from jax.sharding import Mesh, PartitionSpec as P

D = 256
H = 8
K = 8
HITS = 2
CAM_ROWS = 1024
Q = 512
CAM_DEVICES = 8
ZY_DEVICES = 16

BLOCK = 24
STRIPE = CAM_DEVICES * BLOCK
STRIPES = 6
WINDOW = STRIPES * BLOCK
HALF_WINDOW = WINDOW // 2
CHUNK = 8
LANES = HITS * H * CHUNK
CHUNKS = WINDOW // CHUNK
HALF_CHUNKS = CHUNKS // 2
Q_STEP = 32

whole = pl.BlockSpec(memory_space=pltpu.VMEM)
anywhere = pl.BlockSpec(memory_space=pltpu.HBM)


def listed(i):
    return ((i & 1) ^ 1) * 8 + ((i >> 1) ^ 4)


def device_at(place):
    return ((place & 7) ^ 4) * 2 + ((place >> 3) ^ 1)


def cam_listed(i, core):
    return i ^ (7 - core)


def first_stripe(camera):
    return (camera * 16) // 3


def mix_kernel(
    hit_any, index_any, attention_any, validity_any, mix_ref, starts_ref,
    hit_ref, index_ref, attention_ref, validity_ref, row_ref, weight_ref, sems,
):
    copies = [
        pltpu.make_async_copy(source, target, sems.at[i])
        for i, (source, target) in enumerate(
            (
                (index_any, index_ref),
                (attention_any, attention_ref),
                (validity_any, validity_ref),
                (hit_any, hit_ref),
            )
        )
    ]
    for copy in copies:
        copy.start()
    for copy in copies:
        copy.wait()
    core, cam = lax.axis_index("core"), lax.axis_index("cam")
    hit_count = validity_ref[0:1, :] + validity_ref[1:2, :]
    inverse = 1.0 / jnp.maximum(hit_count, 1).astype(jnp.float32)
    attention = attention_ref[...].astype(jnp.float32)
    rows, weights = [], []
    for slot in range(HITS):
        camera = hit_ref[0, slot]
        shifted = index_ref[slot] + (camera * CAM_ROWS - first_stripe(camera) * STRIPE)
        stripe = (shifted * 683) >> 17
        within = shifted - stripe * STRIPE
        owner = (within * 171) >> 12
        row = within - owner * BLOCK + (stripe >> 1) * BLOCK
        other = ((stripe + first_stripe(camera)) & 1) != core
        row = jnp.where(other, row + HALF_WINDOW, row)
        row = jnp.where(owner == cam, row, -1)
        rows.append(row.astype(jnp.float32))
        weights.append(attention * validity_ref[slot : slot + 1, :].astype(jnp.float32) * inverse)
    rows = jnp.concatenate(rows, axis=0).T.astype(jnp.bfloat16)
    weights = jnp.concatenate(weights, axis=0).T.astype(jnp.bfloat16)
    source = lax.broadcasted_iota(jnp.int32, (HITS * H * K, LANES), 0)
    group = lax.broadcasted_iota(jnp.int32, (HITS * H * K, LANES), 1) // CHUNK
    for k in range(K):
        spread = (source == group * K + k).astype(jnp.bfloat16)
        spread_rows = jnp.dot(rows, spread, preferred_element_type=jnp.float32)
        row_ref[k] = spread_rows.astype(jnp.int32).astype(jnp.int16)
        spread_weights = jnp.dot(weights, spread, preferred_element_type=jnp.float32)
        weight_ref[k] = spread_weights.astype(jnp.bfloat16)

    for half, parity in enumerate((core, 1 - core)):
        for slot in range(HITS):
            first = (first_stripe(hit_ref[0, slot]) + 1 - parity) // 2
            for i in range(STRIPES // 2):
                line = (half * HITS + slot) * (STRIPES // 2) + i
                starts_ref[line : line + 1, :] = jnp.full((1, LANES), listed(first + i) * BLOCK, jnp.int32)

    local = lax.broadcasted_iota(jnp.int32, (Q_STEP, LANES), 1) % CHUNK

    @pl.loop(0, Q // Q_STEP)
    def _(step):
        part = pl.ds(pl.multiple_of(step * Q_STEP, Q_STEP), Q_STEP)
        picked = [row_ref[k, part, :] for k in range(K)]
        scale = [weight_ref[k, part, :] for k in range(K)]
        for chunk in range(CHUNKS):
            target = (local + chunk * CHUNK).astype(jnp.int16)
            total = jnp.zeros((Q_STEP, LANES), jnp.bfloat16)
            for k in range(K):
                total = jnp.where(picked[k] == target, scale[k], total)
            mix_ref[part, chunk * LANES : (chunk + 1) * LANES] = total.astype(jnp.bfloat16)


def build_mix(hit_list, index, attention, validity):
    inputs = (pltpu.with_memory_space_constraint(x, pltpu.HBM) for x in (hit_list, index, attention, validity))
    return pl.pallas_call(
        mix_kernel,
        out_shape=(
            jax.ShapeDtypeStruct((Q, CHUNKS * LANES), jnp.bfloat16),
            jax.ShapeDtypeStruct((HITS * STRIPES, LANES), jnp.int32),
        ),
        in_specs=[anywhere, anywhere, anywhere, anywhere],
        out_specs=(whole, whole),
        scratch_shapes=[
            pltpu.SMEM((1, HITS), jnp.int32),
            pltpu.VMEM((HITS, H * K, Q), jnp.int32),
            pltpu.VMEM((H * K, Q), jnp.bfloat16),
            pltpu.VMEM((HITS, Q), jnp.int32),
            pltpu.VMEM((K, Q, LANES), jnp.int16),
            pltpu.VMEM((K, Q, LANES), jnp.bfloat16),
            pltpu.SemaphoreType.DMA((4,)),
        ],
        compiler_params=pltpu.CompilerParams(vmem_limit_bytes=16 << 20),
        cost_estimate=pl.CostEstimate(flops=1 << 29, bytes_accessed=4 << 20, transcendentals=0),
        name="build_mix",
    )(*inputs)


def mixed(starts_ref, gathered_ref, half, weight_ref, mix, spread_ref):
    windows = []
    for slot in range(HITS):
        for i in range(STRIPES // 2):
            start = pl.multiple_of(starts_ref[(half * HITS + slot) * (STRIPES // 2) + i, 0], 8)
            windows.append(gathered_ref[pl.ds(start, BLOCK), :])
    features = jnp.concatenate(windows, axis=0)
    values = jnp.dot(features, weight_ref[...], preferred_element_type=jnp.float32)
    head_of_row = (lax.broadcasted_iota(jnp.int32, (LANES, D), 0) // CHUNK) % H
    head_of_column = lax.broadcasted_iota(jnp.int32, (LANES, D), 1) // (D // H)
    same_head = head_of_row == head_of_column
    for chunk in range(HALF_CHUNKS):
        pieces = []
        for slot in range(HITS):
            first = slot * HALF_WINDOW + chunk * CHUNK
            pieces += [values[first : first + CHUNK, :]] * H
        tall = jnp.where(same_head, jnp.concatenate(pieces, axis=0), 0.0)
        spread_ref[chunk * LANES : (chunk + 1) * LANES, :] = tall.astype(jnp.bfloat16)
    return jnp.dot(mix, spread_ref[...], preferred_element_type=jnp.float32)


def near_kernel(starts_ref, mine_ref, weight_ref, mix_ref, out_ref, spread_ref):
    out_ref[...] = mixed(starts_ref, mine_ref, 0, weight_ref, mix_ref[:, : HALF_CHUNKS * LANES], spread_ref)


def far_kernel(starts_ref, other_ref, weight_ref, mix_ref, near_ref, out_ref, spread_ref):
    total = near_ref[...] + mixed(
        starts_ref, other_ref, 1, weight_ref, mix_ref[:, HALF_CHUNKS * LANES :], spread_ref
    )
    total = total.astype(jnp.bfloat16)
    share = Q // CAM_DEVICES
    core = lax.axis_index("core")
    for i in range(CAM_DEVICES):
        out_ref[cam_listed(i, core)] = total[i * share : (i + 1) * share, :]


def sample(kernel, name, out_shape, *operands):
    return pl.pallas_call(
        kernel,
        out_shape=out_shape,
        in_specs=[whole] * len(operands),
        out_specs=whole,
        scratch_shapes=[pltpu.VMEM((HALF_CHUNKS * LANES, D), jnp.bfloat16)],
        compiler_params=pltpu.CompilerParams(vmem_limit_bytes=16 << 20),
        cost_estimate=pl.CostEstimate(flops=1 << 28, bytes_accessed=1 << 20, transcendentals=0),
        name=name,
    )(*operands)


def project_kernel(pieces_ref, weight_ref, out_ref):
    total = pieces_ref[0].astype(jnp.float32)
    for i in range(1, CAM_DEVICES):
        total = total + pieces_ref[i].astype(jnp.float32)
    out_ref[...] = jnp.dot(
        total.astype(jnp.bfloat16), weight_ref[...], preferred_element_type=jnp.float32
    ).astype(jnp.bfloat16)


def project(pieces, output_weight):
    return pl.pallas_call(
        project_kernel,
        out_shape=jax.ShapeDtypeStruct((Q // CAM_DEVICES, D), jnp.bfloat16),
        in_specs=[whole, whole],
        out_specs=whole,
        compiler_params=pltpu.CompilerParams(vmem_limit_bytes=8 << 20),
        name="project",
    )(pieces, output_weight)


def swapped(x, axis):
    return lax.ppermute(x, axis, [(0, 1), (1, 0)])


def body(features, value_weight, output_weight, hit_list, sample_index, attention, validity):
    copies = jnp.broadcast_to(features[None], (ZY_DEVICES, BLOCK, D))
    mine = lax.all_to_all(
        copies, "zy", 0, 0, tiled=True, axis_index_groups=[[device_at(i) for i in range(ZY_DEVICES)]]
    ).reshape(ZY_DEVICES * BLOCK, D)
    mix, starts = build_mix(hit_list, sample_index.transpose(1, 2, 0), attention.T, validity.T)
    mine, mix, starts = lax.optimization_barrier((mine, mix, starts))
    other = swapped(mine, "core")
    near_shape = jax.ShapeDtypeStruct((Q, D), jnp.float32)
    near = sample(near_kernel, "sample_near", near_shape, starts, mine, value_weight, mix)
    pieces_shape = jax.ShapeDtypeStruct((CAM_DEVICES, Q // CAM_DEVICES, D), jnp.bfloat16)
    pieces = sample(far_kernel, "sample_far", pieces_shape, starts, other, value_weight, mix, near)
    groups = [
        [(zy * 2 + core) * CAM_DEVICES + cam_listed(i, core) for i in range(CAM_DEVICES)]
        for zy in range(ZY_DEVICES)
        for core in range(2)
    ]
    arrived = lax.all_to_all(pieces, ("zy", "core", "cam"), 0, 0, tiled=True, axis_index_groups=groups)
    return project(arrived, output_weight)


def solution(mesh):
    split = Mesh(mesh.devices.reshape(ZY_DEVICES, 2, CAM_DEVICES), ("zy", "core", "cam"))
    tile = ("zy", "core")
    every = tile + ("cam",)
    in_specs = (
        P(every, None),
        P(),
        P(),
        P(tile, None),
        P(tile, None, None),
        P(tile, None),
        P(tile, None),
    )
    return jax.shard_map(body, mesh=split, in_specs=in_specs, out_specs=P(every, None), check_vma=False)
```
